32 devices in a mesh: groups: 2 (over y), rows: 4 (over z), sub: 2 (over x), cols: 2 (over core).
Axes of the slice: x: 2, y: 2, z: 4, core: 2. Of those that a mesh axis runs over, the one named last changes fastest.
Arguments:
- noise: bfloat16 [16384, 256], P(('groups', 'rows', 'sub'), 'cols'), parts along dimension 0, may hold values from -6 to 6
- bases: bfloat16 [2, 16384, 256], P(None, ('groups', 'rows', 'sub')), parts along dimension 1, may hold values from -0.375 to 0.375
- cores: bfloat16 [6, 256, 256], P('groups'), parts along dimension 0, may hold values from -0.09375 to 0.09375
- self_mob: float32 [16384], P(('groups', 'rows', 'sub')), parts along dimension 0, may hold values from 0.5 to 2
Outputs:
- displace: float32 [16384, 256], P(('groups', 'rows', 'sub'), 'cols'), parts along dimension 0
The draws below stay inside these ranges and needn't reach their ends.
There are 2 independent parts, one for each index of `groups`. The reference program is written for one: setup_inputs(seed, part) draws one part's arguments, and reference() takes and returns one part's arrays. A program takes and returns all parts, laid end to end along the dimension named above; each array names one. Nothing has to cross between parts.
All inputs are finite; a program needn't handle non-finite values.
Results may differ from the reference program's by a relative error of at most 0.0022.
Values may be sent and summed in bfloat16 or wider, within the bound.
No kernel may reach another device: no remote copies, remote signals or barrier semaphores. Data moves between devices by JAX's collectives and lax.ppermute only.
A program may use at most 64 MiB of HBM per device.

```python
import math
import jax
import jax.numpy as jnp
from jax import lax

K = 256
COLS = 256
LEVELS = 2
PAIRS = 3
BEADS = 8192


def block_levels(own_key, shape, split, low, high):
    level, own = 1.0, jax.random.fold_in(own_key, 6)
    for dim, parts in split:
        heights = jnp.exp(jax.random.uniform(jax.random.fold_in(own, dim), (parts,), jnp.float32, low / len(split), high / len(split)))
        level = level * jnp.repeat(heights, shape[dim] // parts).reshape([-1 if axis == dim else 1 for axis in range(len(shape))])
    return level


def gaussian(key, extent, scale, most, split=(), kind=jnp.bfloat16):
    array = jax.random.normal(key, extent, jnp.float32) * scale
    if len(split) > 0:
        array = block_levels(key, extent, split, -0.22, 0.18) * array
    return jnp.clip(array, min=-most, max=most).astype(kind)


def setup_inputs(seed: int = 0, part: int = 0) -> dict:
    key_list = jax.random.split(jax.random.key(seed), 5)
    part_keys = jax.random.split(jax.random.fold_in(key_list[4], part), 5)
    return {
        "noise": gaussian(part_keys[0], (BEADS, COLS), 1.0, 6.0, ((0, 8), (1, 2))),
        "bases": gaussian(part_keys[1], (LEVELS, BEADS, K), K ** -0.5, 0.375, ((1, 8),)),
        "cores": gaussian(part_keys[2], (PAIRS, K, K), (BEADS // 2) ** -0.5, 0.09375),
        "self_mob": jnp.clip(jnp.exp(math.log(2.0) - 1.3862944 * jax.random.uniform(part_keys[3], (BEADS,), jnp.float32) ** block_levels(part_keys[3], (BEADS,), ((0, 8),), -0.2, 0.2)), 0.5, 2.0),
    }


def reference(noise, bases, cores, self_mob):
    total = noise.shape[0]
    rank = bases.shape[2]
    width = noise.shape[1]
    result = self_mob[:, None] * noise.astype(jnp.float32)
    for level in range(1, LEVELS + 1):
        nodes = 2 ** level
        size = total // nodes
        basis = bases[level - 1].reshape(nodes, size, rank).astype(jnp.float32)
        signal = noise.reshape(nodes, size, width).astype(jnp.float32)
        proj = jnp.einsum('nsk,nsc->nkc', basis, signal, precision=lax.Precision.HIGHEST)
        other = proj.reshape(nodes // 2, 2, rank, width)[:, ::-1].reshape(nodes, rank, width)
        chosen = cores[2 ** (level - 1) - 1:2 ** level - 1].astype(jnp.float32)
        paired = jnp.stack([chosen, jnp.transpose(chosen, (0, 2, 1))], axis=1).reshape(nodes, rank, rank)
        mapped = jnp.einsum('nij,njc->nic', paired, other, precision=lax.Precision.HIGHEST)
        mapped = mapped.astype(jnp.bfloat16).astype(jnp.float32)
        added = jnp.einsum('nsk,nkc->nsc', basis, mapped, precision=lax.Precision.HIGHEST)
        result = result + added.reshape(total, width)
    return result
```

```python
import jax
import jax.numpy as jnp
from jax import lax
from jax.sharding import PartitionSpec as P


def exchange(value, row_mask, sub_mask):
    subs = lax.axis_size("sub")
    count = lax.axis_size("rows") * subs
    mask = row_mask * subs + sub_mask
    return lax.ppermute(value, ("rows", "sub"), [(i, i ^ mask) for i in range(count)])


def group_sum(value, bits):
    while bits:
        now, bits = bits[:2], bits[2:]
        masks = list(now)
        if len(now) == 2:
            masks.append((now[0][0] ^ now[1][0], now[0][1] ^ now[1][1]))
        parts = [exchange(value, *mask) for mask in masks]
        total = value.astype(jnp.float32)
        for part in parts:
            total = total + part.astype(jnp.float32)
        value = total
    return value.astype(jnp.float32)


def per_device(noise, bases, cores, self_mob):
    depth = lax.axis_size("rows").bit_length() - 1
    sub_bits = lax.axis_size("sub").bit_length() - 1
    place = lax.axis_index("rows")
    result = self_mob[:, None] * noise.astype(jnp.float32)
    for level in range(1, bases.shape[0] + 1):
        basis = bases[level - 1]
        proj = jnp.einsum("rc,rk->ck", noise, basis, preferred_element_type=jnp.float32)
        bit = depth - level
        other = exchange(proj.astype(jnp.bfloat16), 2**bit, 0)
        bits = [(0, 2**b) for b in range(sub_bits)] + [(2**b, 0) for b in range(bit)]
        other = group_sum(other, bits)
        node = place // 2**bit
        core = lax.dynamic_index_in_dim(cores, 2 ** (level - 1) - 1 + node // 2, 0, keepdims=False)
        mixer = jnp.where(node % 2 == 1, core, core.T).astype(jnp.float32)
        mapped = jnp.dot(other, mixer, precision=lax.Precision.HIGHEST).astype(jnp.bfloat16)
        result = result + jnp.einsum("rk,ck->rc", basis, mapped, preferred_element_type=jnp.float32)
    return result


def solution(mesh):
    in_specs = (
        P(("groups", "rows", "sub"), "cols"),
        P(None, ("groups", "rows", "sub"), None),
        P("groups", None, None),
        P(("groups", "rows", "sub")),
    )
    out_specs = P(("groups", "rows", "sub"), "cols")
    return jax.shard_map(
        per_device, mesh=mesh, in_specs=in_specs, out_specs=out_specs, check_vma=False
    )
```

```python
import functools

import jax
import jax.numpy as jnp
from jax import lax
from jax.experimental import pallas as pl
from jax.experimental.pallas import tpu as pltpu
from jax.sharding import PartitionSpec as P

VMEM = pl.BlockSpec(memory_space=pltpu.VMEM)
HBM = pl.BlockSpec(memory_space=pltpu.HBM)
ANY = pl.BlockSpec(memory_space=pl.ANY)
PARAMS = pltpu.CompilerParams(vmem_limit_bytes=8 * 2**20)
CHUNKS = 4


def f32(value):
    return value.astype(jnp.float32)


def cost(flops, bytes_accessed):
    return pl.CostEstimate(flops=flops, bytes_accessed=bytes_accessed, transcendentals=0)


def exchange(value, row_mask, sub_mask, col_mask):
    subs, cols = lax.axis_size("sub"), lax.axis_size("cols")
    count = lax.axis_size("rows") * subs * cols
    mask = (row_mask * subs + sub_mask) * cols + col_mask
    return lax.ppermute(value, ("rows", "sub", "cols"), [(i, i ^ mask) for i in range(count)])


def project_onto(noise, basis):
    return lax.dot_general(
        noise, basis, (((0,), (0,)), ((), ())), preferred_element_type=jnp.float32
    ).astype(jnp.bfloat16)


def load_kernel(noise_hbm, bases_hbm, noise_ref, bases_ref, out_ref, sems):
    count = bases_ref.shape[0]
    copies = [pltpu.make_async_copy(noise_hbm, noise_ref, sems.at[count])]
    copies += [
        pltpu.make_async_copy(bases_hbm.at[level], bases_ref.at[level], sems.at[level])
        for level in range(count)
    ]
    for copy in copies:
        copy.start()
    copies[0].wait()
    copies[1].wait()
    out_ref[...] = project_onto(noise_ref[...], bases_ref[0])
    for copy in copies[2:]:
        copy.wait()


def load(noise, bases):
    size, cols = noise.shape
    count, _, rank = bases.shape
    return pl.pallas_call(
        load_kernel,
        out_shape=(
            jax.ShapeDtypeStruct(noise.shape, noise.dtype),
            jax.ShapeDtypeStruct(bases.shape, bases.dtype),
            jax.ShapeDtypeStruct((cols, rank), jnp.bfloat16),
        ),
        in_specs=[HBM, HBM],
        out_specs=(VMEM, VMEM, VMEM),
        scratch_shapes=[pltpu.SemaphoreType.DMA((count + 1,))],
        compiler_params=PARAMS,
        cost_estimate=cost(2 * size * cols * rank, 2 * size * (cols + count * rank)),
    )(
        pltpu.with_memory_space_constraint(noise, pltpu.HBM),
        pltpu.with_memory_space_constraint(bases, pltpu.HBM),
    )


def project_kernel(level, noise_ref, bases_ref, out_ref):
    out_ref[...] = project_onto(noise_ref[...], bases_ref[level])


def project(noise, bases, level):
    size, cols = noise.shape
    rank = bases.shape[2]
    return pl.pallas_call(
        functools.partial(project_kernel, level),
        out_shape=jax.ShapeDtypeStruct((cols, rank), jnp.bfloat16),
        in_specs=[VMEM, VMEM],
        out_specs=VMEM,
        compiler_params=PARAMS,
        cost_estimate=cost(2 * size * cols * rank, 2 * size * (cols + rank)),
    )(noise, bases)


def mixer_kernel(depth, cores_ref, out_ref):
    place = lax.axis_index("rows")
    for level in range(out_ref.shape[0]):
        node = place // 2 ** (depth - level - 1)
        core = cores_ref[2**level - 1 + node // 2]

        @pl.when(node % 2 == 1)
        def _():
            out_ref[level] = core

        @pl.when(node % 2 == 0)
        def _():
            out_ref[level] = core.T


def halves(value):
    high = value.astype(jnp.bfloat16)
    return jnp.concatenate([high, (value - f32(high)).astype(jnp.bfloat16)], axis=0)


def mapped(mixer, part_refs):
    total = f32(part_refs[0][...])
    for ref in part_refs[1:]:
        total = total + f32(ref[...])
    both = jnp.dot(halves(total), mixer, preferred_element_type=jnp.float32)
    cols = total.shape[0]
    return halves(both[:cols] + both[cols:])


def spread(basis, weights):
    both = lax.dot_general(
        basis, weights, (((1,), (1,)), ((), ())), preferred_element_type=jnp.float32
    )
    cols = weights.shape[0] // 2
    return both[:, :cols] + both[:, cols:]


def first_kernel(level, noise_ref, mob_ref, bases_ref, mixer_ref, *refs):
    part_refs, out_ref = refs[:-1], refs[-1]
    weights = mapped(mixer_ref[level], part_refs)
    mob = mob_ref[...].T
    rows = mob.shape[0]
    for i in range(mob.shape[1]):
        part = pl.ds(i * rows, rows)
        out_ref[part, :] = mob[:, i : i + 1] * f32(noise_ref[part, :]) + spread(
            bases_ref[level, part, :], weights
        )


def next_kernel(level, sum_ref, bases_ref, mixer_ref, *refs):
    part_refs, out_ref = refs[:-1], refs[-1]
    out_ref[...] = sum_ref[...] + spread(bases_ref[level], mapped(mixer_ref[level], part_refs))


def last_kernel(level, sum_ref, bases_ref, mixer_ref, *refs):
    part_refs, out_hbm, buf, sems = refs[:-3], refs[-3], refs[-2], refs[-1]
    weights = mapped(mixer_ref[level], part_refs)
    rows = buf.shape[0] // CHUNKS
    copies = []
    for i in range(CHUNKS):
        part = pl.ds(i * rows, rows)
        buf[part, :] = sum_ref[part, :] + spread(bases_ref[level, part, :], weights)
        copies.append(pltpu.make_async_copy(buf.at[part], out_hbm.at[part], sems.at[i]))
        copies[-1].start()
    for copy in copies:
        copy.wait()


def gather(level, proj, depth, sub_bits):
    swap = 2 ** (depth - level - 1)
    bits = [(0, 2**b) for b in range(sub_bits)] + [(2**b, 0) for b in range(depth - level - 1)]
    if level > 0 and len(bits) < 2:
        return [
            exchange(proj, swap ^ row_mask, sub_mask, 0)
            for row_mask, sub_mask in [(0, 0)] + bits
        ]
    flip = lax.axis_size("cols") - 1
    value = exchange(proj, swap, 0, flip)
    if not bits:
        return [exchange(value, 0, 0, flip) if flip else value]
    while bits:
        now, bits = bits[:2], bits[2:]
        masks = list(now)
        if len(now) == 2:
            masks.append((now[0][0] ^ now[1][0], now[0][1] ^ now[1][1]))
        terms = [exchange(value, *mask, flip) for mask in masks]
        terms.append(exchange(value, 0, 0, flip) if flip else value)
        if bits:
            value, flip = sum(f32(term) for term in terms), 0
    return terms


def per_device(noise, bases, cores, self_mob):
    depth = lax.axis_size("rows").bit_length() - 1
    sub_bits = lax.axis_size("sub").bit_length() - 1
    size, cols = noise.shape
    count, _, rank = bases.shape
    lanes = 128
    noise, bases, first = load(noise, bases)
    parts = []
    for level in range(count):
        proj = project(noise, bases, level) if level else first
        parts.append(gather(level, proj, depth, sub_bits))
    mixer = pl.pallas_call(
        functools.partial(mixer_kernel, depth),
        out_shape=jax.ShapeDtypeStruct((count, *cores.shape[1:]), cores.dtype),
        in_specs=[VMEM],
        out_specs=VMEM,
        compiler_params=PARAMS,
        cost_estimate=cost(0, cores.size * 4),
    )(cores)
    shape = jax.ShapeDtypeStruct((size, cols), jnp.float32)
    estimate = cost(4 * size * cols * rank, size * cols * 8)
    result = None
    for level in range(count - 1, 0, -1):
        if result is None:
            kernel, operands = first_kernel, (noise, self_mob.reshape(size // lanes, lanes))
        else:
            kernel, operands = next_kernel, (result,)
        operands += (bases, mixer, *parts[level])
        result = pl.pallas_call(
            functools.partial(kernel, level),
            out_shape=shape,
            in_specs=[VMEM] * len(operands),
            out_specs=VMEM,
            compiler_params=PARAMS,
            cost_estimate=estimate,
        )(*operands)
    if result is None:
        result = self_mob[:, None] * f32(noise)
    operands = (result, bases, mixer, *parts[0])
    return pl.pallas_call(
        functools.partial(last_kernel, 0),
        out_shape=shape,
        in_specs=[VMEM] * len(operands),
        out_specs=ANY,
        scratch_shapes=[pltpu.VMEM((size, cols), jnp.float32), pltpu.SemaphoreType.DMA((CHUNKS,))],
        compiler_params=PARAMS,
        cost_estimate=estimate,
    )(*operands)


def solution(mesh):
    in_specs = (
        P(("groups", "rows", "sub"), "cols"),
        P(None, ("groups", "rows", "sub"), None),
        P("groups", None, None),
        P(("groups", "rows", "sub")),
    )
    out_specs = P(("groups", "rows", "sub"), "cols")
    return jax.shard_map(
        per_device, mesh=mesh, in_specs=in_specs, out_specs=out_specs, check_vma=False
    )
```

```python
import functools

import jax
import jax.numpy as jnp
from jax import lax
from jax.experimental import pallas as pl
from jax.experimental.pallas import tpu as pltpu
from jax.sharding import PartitionSpec as P

VMEM = pl.BlockSpec(memory_space=pltpu.VMEM)
HBM = pl.BlockSpec(memory_space=pltpu.HBM)
ANY = pl.BlockSpec(memory_space=pl.ANY)
PARAMS = pltpu.CompilerParams(vmem_limit_bytes=8 * 2**20)
CHUNKS = 4


def f32(value):
    return value.astype(jnp.float32)


def cost(flops, bytes_accessed):
    return pl.CostEstimate(flops=flops, bytes_accessed=bytes_accessed, transcendentals=0)


def exchange(value, row_mask, sub_mask, col_mask):
    subs, cols = lax.axis_size("sub"), lax.axis_size("cols")
    count = lax.axis_size("rows") * subs * cols
    mask = (row_mask * subs + sub_mask) * cols + col_mask
    return lax.ppermute(value, ("rows", "sub", "cols"), [(i, i ^ mask) for i in range(count)])


def project_onto(noise, basis):
    return lax.dot_general(
        noise, basis, (((0,), (0,)), ((), ())), preferred_element_type=jnp.float32
    )


def load_kernel(noise_hbm, bases_hbm, noise_ref, bases_ref, out_ref, wide_ref, sems):
    count = bases_ref.shape[0]
    copies = [pltpu.make_async_copy(noise_hbm, noise_ref, sems.at[count])]
    copies += [
        pltpu.make_async_copy(bases_hbm.at[level], bases_ref.at[level], sems.at[level])
        for level in range(count)
    ]
    for copy in copies:
        copy.start()
    copies[0].wait()
    copies[1].wait()
    proj = project_onto(noise_ref[...], bases_ref[0])
    out_ref[...] = proj.astype(out_ref.dtype)
    wide_ref[...] = proj
    for copy in copies[2:]:
        copy.wait()


def load(noise, bases):
    size, cols = noise.shape
    count, _, rank = bases.shape
    return pl.pallas_call(
        load_kernel,
        out_shape=(
            jax.ShapeDtypeStruct(noise.shape, noise.dtype),
            jax.ShapeDtypeStruct(bases.shape, bases.dtype),
            jax.ShapeDtypeStruct((cols, rank), jnp.bfloat16),
            jax.ShapeDtypeStruct((cols, rank), jnp.float32),
        ),
        in_specs=[HBM, HBM],
        out_specs=(VMEM, VMEM, VMEM, VMEM),
        scratch_shapes=[pltpu.SemaphoreType.DMA((count + 1,))],
        compiler_params=PARAMS,
        cost_estimate=cost(2 * size * cols * rank, 2 * size * (cols + count * rank)),
    )(
        pltpu.with_memory_space_constraint(noise, pltpu.HBM),
        pltpu.with_memory_space_constraint(bases, pltpu.HBM),
    )


def project_kernel(level, noise_ref, bases_ref, out_ref):
    out_ref[...] = project_onto(noise_ref[...], bases_ref[level]).astype(out_ref.dtype)


def project(noise, bases, level):
    size, cols = noise.shape
    rank = bases.shape[2]
    return pl.pallas_call(
        functools.partial(project_kernel, level),
        out_shape=jax.ShapeDtypeStruct((cols, rank), jnp.bfloat16),
        in_specs=[VMEM, VMEM],
        out_specs=VMEM,
        compiler_params=PARAMS,
        cost_estimate=cost(2 * size * cols * rank, 2 * size * (cols + rank)),
    )(noise, bases)


def mixer_kernel(depth, cores_ref, out_ref):
    place = lax.axis_index("rows")
    for level in range(out_ref.shape[0]):
        node = place // 2 ** (depth - level - 1)
        core = cores_ref[2**level - 1 + node // 2]

        @pl.when(node % 2 == 1)
        def _():
            out_ref[level] = core

        @pl.when(node % 2 == 0)
        def _():
            out_ref[level] = core.T


def halves(value):
    high = value.astype(jnp.bfloat16)
    return jnp.concatenate([high, (value - f32(high)).astype(jnp.bfloat16)], axis=0)


def mapped(mixer, part_refs):
    total = f32(part_refs[0][...])
    for ref in part_refs[1:]:
        total = total + f32(ref[...])
    both = jnp.dot(halves(total), mixer, preferred_element_type=jnp.float32)
    cols = total.shape[0]
    return halves(both[:cols] + both[cols:])


def spread(basis, weights):
    both = lax.dot_general(
        basis, weights, (((1,), (1,)), ((), ())), preferred_element_type=jnp.float32
    )
    cols = weights.shape[0] // 2
    return both[:, :cols] + both[:, cols:]


def first_kernel(level, noise_ref, mob_ref, bases_ref, mixer_ref, *refs):
    part_refs, out_ref = refs[:-1], refs[-1]
    weights = mapped(mixer_ref[level], part_refs)
    mob = mob_ref[...].T
    rows = mob.shape[0]
    for i in range(mob.shape[1]):
        part = pl.ds(i * rows, rows)
        out_ref[part, :] = mob[:, i : i + 1] * f32(noise_ref[part, :]) + spread(
            bases_ref[level, part, :], weights
        )


def next_kernel(level, sum_ref, bases_ref, mixer_ref, *refs):
    part_refs, out_ref = refs[:-1], refs[-1]
    out_ref[...] = sum_ref[...] + spread(bases_ref[level], mapped(mixer_ref[level], part_refs))


def last_kernel(level, sum_ref, bases_ref, mixer_ref, *refs):
    part_refs, out_hbm, buf, sems = refs[:-3], refs[-3], refs[-2], refs[-1]
    weights = mapped(mixer_ref[level], part_refs)
    rows = buf.shape[0] // CHUNKS
    copies = []
    for i in range(CHUNKS):
        part = pl.ds(i * rows, rows)
        buf[part, :] = sum_ref[part, :] + spread(bases_ref[level, part, :], weights)
        copies.append(pltpu.make_async_copy(buf.at[part], out_hbm.at[part], sems.at[i]))
        copies[-1].start()
    for copy in copies:
        copy.wait()


def gather(level, proj, wide, depth, sub_bits):
    swap = 2 ** (depth - level - 1)
    bits = [(0, 2**b) for b in range(sub_bits)] + [(2**b, 0) for b in range(depth - level - 1)]
    if level > 0 and len(bits) < 2:
        return [
            exchange(proj, swap ^ row_mask, sub_mask, 0)
            for row_mask, sub_mask in [(0, 0)] + bits
        ]
    flip = lax.axis_size("cols") - 1
    value = proj
    own = exchange(wide, 0, 0, flip) if flip else wide
    cross, step = flip, 0
    while bits:
        now, bits = bits[:2], bits[2:]
        masks = list(now)
        if len(now) == 2:
            masks.append((now[0][0] ^ now[1][0], now[0][1] ^ now[1][1]))
        terms = [f32(exchange(value, *mask, cross)) for mask in reversed(masks)]
        own = sum(terms[1:], terms[0]) + f32(own)
        value, cross = own, 0
        step += 1
    total = f32(own)
    return [exchange(total.astype(jnp.bfloat16), swap, 0, flip)]


def per_device(noise, bases, cores, self_mob):
    depth = lax.axis_size("rows").bit_length() - 1
    sub_bits = lax.axis_size("sub").bit_length() - 1
    size, cols = noise.shape
    count, _, rank = bases.shape
    lanes = 128
    noise, bases, first, wide = load(noise, bases)
    parts = []
    for level in range(count):
        proj = project(noise, bases, level) if level else first
        parts.append(gather(level, proj, proj if level else wide, depth, sub_bits))
    mixer = pl.pallas_call(
        functools.partial(mixer_kernel, depth),
        out_shape=jax.ShapeDtypeStruct((count, *cores.shape[1:]), cores.dtype),
        in_specs=[VMEM],
        out_specs=VMEM,
        compiler_params=PARAMS,
        cost_estimate=cost(0, cores.size * 4),
    )(cores)
    shape = jax.ShapeDtypeStruct((size, cols), jnp.float32)
    estimate = cost(4 * size * cols * rank, size * cols * 8)
    result = None
    for level in range(count - 1, 0, -1):
        if result is None:
            kernel, operands = first_kernel, (noise, self_mob.reshape(size // lanes, lanes))
        else:
            kernel, operands = next_kernel, (result,)
        operands += (bases, mixer, *parts[level])
        result = pl.pallas_call(
            functools.partial(kernel, level),
            out_shape=shape,
            in_specs=[VMEM] * len(operands),
            out_specs=VMEM,
            compiler_params=PARAMS,
            cost_estimate=estimate,
        )(*operands)
    if result is None:
        result = self_mob[:, None] * f32(noise)
    operands = (result, bases, mixer, *parts[0])
    return pl.pallas_call(
        functools.partial(last_kernel, 0),
        out_shape=shape,
        in_specs=[VMEM] * len(operands),
        out_specs=ANY,
        scratch_shapes=[pltpu.VMEM((size, cols), jnp.float32), pltpu.SemaphoreType.DMA((CHUNKS,))],
        compiler_params=PARAMS,
        cost_estimate=estimate,
    )(*operands)


def solution(mesh):
    in_specs = (
        P(("groups", "rows", "sub"), "cols"),
        P(None, ("groups", "rows", "sub"), None),
        P("groups", None, None),
        P(("groups", "rows", "sub")),
    )
    out_specs = P(("groups", "rows", "sub"), "cols")
    return jax.shard_map(
        per_device, mesh=mesh, in_specs=in_specs, out_specs=out_specs, check_vma=False
    )
```

```python
import functools

import jax
import jax.numpy as jnp
from jax import lax
from jax.experimental import pallas as pl
from jax.experimental.pallas import tpu as pltpu
from jax.sharding import PartitionSpec as P

VMEM = pl.BlockSpec(memory_space=pltpu.VMEM)
HBM = pl.BlockSpec(memory_space=pltpu.HBM)
ANY = pl.BlockSpec(memory_space=pl.ANY)
PARAMS = pltpu.CompilerParams(vmem_limit_bytes=8 * 2**20)
CHUNKS = 4


def f32(value):
    return value.astype(jnp.float32)


def cost(flops, bytes_accessed):
    return pl.CostEstimate(flops=flops, bytes_accessed=bytes_accessed, transcendentals=0)


def exchange(value, low_mask, high_mask, col_mask):
    rows, subs, cols = (lax.axis_size(axis) for axis in ("rows", "sub", "cols"))
    pairs = []
    for i in range(rows * subs * cols):
        row_mask, sub_mask = low_mask if i < rows * subs * cols // 2 else high_mask
        pairs.append((i, i ^ ((row_mask * subs + sub_mask) * cols + col_mask)))
    return lax.ppermute(value, ("rows", "sub", "cols"), pairs)


def project_onto(noise, basis):
    return lax.dot_general(
        noise, basis, (((0,), (0,)), ((), ())), preferred_element_type=jnp.float32
    )


def load_kernel(noise_hbm, bases_hbm, noise_ref, bases_ref, out_ref, wide_ref, sems):
    count = bases_ref.shape[0]
    copies = [pltpu.make_async_copy(noise_hbm, noise_ref, sems.at[count])]
    copies += [
        pltpu.make_async_copy(bases_hbm.at[level], bases_ref.at[level], sems.at[level])
        for level in range(count)
    ]
    for copy in copies:
        copy.start()
    copies[0].wait()
    copies[1].wait()
    proj = project_onto(noise_ref[...], bases_ref[0])
    out_ref[...] = proj.astype(out_ref.dtype)
    wide_ref[...] = proj
    for copy in copies[2:]:
        copy.wait()


def load(noise, bases):
    size, cols = noise.shape
    count, _, rank = bases.shape
    return pl.pallas_call(
        load_kernel,
        out_shape=(
            jax.ShapeDtypeStruct(noise.shape, noise.dtype),
            jax.ShapeDtypeStruct(bases.shape, bases.dtype),
            jax.ShapeDtypeStruct((cols, rank), jnp.bfloat16),
            jax.ShapeDtypeStruct((cols, rank), jnp.float32),
        ),
        in_specs=[HBM, HBM],
        out_specs=(VMEM, VMEM, VMEM, VMEM),
        scratch_shapes=[pltpu.SemaphoreType.DMA((count + 1,))],
        compiler_params=PARAMS,
        cost_estimate=cost(2 * size * cols * rank, 2 * size * (cols + count * rank)),
    )(
        pltpu.with_memory_space_constraint(noise, pltpu.HBM),
        pltpu.with_memory_space_constraint(bases, pltpu.HBM),
    )


def project_kernel(level, noise_ref, bases_ref, out_ref):
    out_ref[...] = project_onto(noise_ref[...], bases_ref[level]).astype(out_ref.dtype)


def project(noise, bases, level):
    size, cols = noise.shape
    rank = bases.shape[2]
    return pl.pallas_call(
        functools.partial(project_kernel, level),
        out_shape=jax.ShapeDtypeStruct((cols, rank), jnp.bfloat16),
        in_specs=[VMEM, VMEM],
        out_specs=VMEM,
        compiler_params=PARAMS,
        cost_estimate=cost(2 * size * cols * rank, 2 * size * (cols + rank)),
    )(noise, bases)


def mixer_kernel(depth, cores_ref, out_ref):
    place = lax.axis_index("rows")
    for level in range(out_ref.shape[0]):
        node = place // 2 ** (depth - level - 1)
        core = cores_ref[2**level - 1 + node // 2]

        @pl.when(node % 2 == 1)
        def _():
            out_ref[level] = core

        @pl.when(node % 2 == 0)
        def _():
            out_ref[level] = core.T


def halves(value):
    high = value.astype(jnp.bfloat16)
    return jnp.concatenate([high, (value - f32(high)).astype(jnp.bfloat16)], axis=0)


def mapped(mixer, part_refs):
    total = f32(part_refs[0][...])
    for ref in part_refs[1:]:
        total = total + f32(ref[...])
    both = jnp.dot(halves(total), mixer, preferred_element_type=jnp.float32)
    cols = total.shape[0]
    return halves(both[:cols] + both[cols:])


def spread(basis, weights):
    both = lax.dot_general(
        basis, weights, (((1,), (1,)), ((), ())), preferred_element_type=jnp.float32
    )
    cols = weights.shape[0] // 2
    return both[:, :cols] + both[:, cols:]


def first_kernel(level, noise_ref, mob_ref, bases_ref, mixer_ref, *refs):
    part_refs, out_ref = refs[:-1], refs[-1]
    weights = mapped(mixer_ref[level], part_refs)
    mob = mob_ref[...].T
    rows = mob.shape[0]
    for i in range(mob.shape[1]):
        part = pl.ds(i * rows, rows)
        out_ref[part, :] = mob[:, i : i + 1] * f32(noise_ref[part, :]) + spread(
            bases_ref[level, part, :], weights
        )


def next_kernel(level, sum_ref, bases_ref, mixer_ref, *refs):
    part_refs, out_ref = refs[:-1], refs[-1]
    out_ref[...] = sum_ref[...] + spread(bases_ref[level], mapped(mixer_ref[level], part_refs))


def fold_kernel(level, bases_ref, mixer_ref, out_ref):
    rank = bases_ref.shape[2]
    folded = lax.dot_general(
        bases_ref[level], mixer_ref[level], (((1,), (1,)), ((), ())), preferred_element_type=jnp.float32
    )
    high = folded.astype(jnp.bfloat16)
    out_ref[:, pl.ds(0, rank)] = high
    out_ref[:, pl.ds(rank, rank)] = (folded - f32(high)).astype(jnp.bfloat16)


def last_kernel(sum_ref, folded_ref, part_ref, out_hbm, buf, sems):
    part = part_ref[...]
    both = jnp.concatenate([part, part], axis=1)
    rows = buf.shape[0] // CHUNKS
    copies = []
    for i in range(CHUNKS):
        here = pl.ds(i * rows, rows)
        buf[here, :] = sum_ref[here, :] + lax.dot_general(
            folded_ref[here, :], both, (((1,), (1,)), ((), ())), preferred_element_type=jnp.float32
        )
        copies.append(pltpu.make_async_copy(buf.at[here], out_hbm.at[here], sems.at[i]))
        copies[-1].start()
    for copy in copies:
        copy.wait()


def gather(level, proj, wide, depth, sub_bits):
    swap = 2 ** (depth - level - 1)
    bits = [(0, 2**b) for b in range(sub_bits)] + [(2**b, 0) for b in range(depth - level - 1)]
    if level > 0 and len(bits) < 2:
        masks = [(swap ^ row_mask, sub_mask) for row_mask, sub_mask in [(0, 0)] + bits]
        return [exchange(proj, mask, mask, 0) for mask in masks]
    flip = lax.axis_size("cols") - 1
    total = exchange(wide, (0, 0), (0, 0), flip) if flip else wide
    value, cross, step = proj, flip, 0
    while bits:
        now, bits = bits[:2], bits[2:]
        low = high = now
        if len(now) == 2:
            both = (now[0][0] ^ now[1][0], now[0][1] ^ now[1][1])
            low, high = (both, now[1], now[0]), (now[0], both, now[1])
        terms = [f32(exchange(value, *masks, cross)) for masks in zip(low, high)]
        total = sum(terms[1:], terms[0]) + f32(total)
        value, cross = total, 0
        step += 1
    mask = (swap, 0)
    return [exchange(f32(total).astype(jnp.bfloat16), mask, mask, flip)]


def per_device(noise, bases, cores, self_mob):
    depth = lax.axis_size("rows").bit_length() - 1
    sub_bits = lax.axis_size("sub").bit_length() - 1
    size, cols = noise.shape
    count, _, rank = bases.shape
    lanes = 128
    noise, bases, first, wide = load(noise, bases)
    parts = []
    for level in range(count):
        proj = project(noise, bases, level) if level else first
        parts.append(gather(level, proj, proj if level else wide, depth, sub_bits))
    mixer = pl.pallas_call(
        functools.partial(mixer_kernel, depth),
        out_shape=jax.ShapeDtypeStruct((count, *cores.shape[1:]), cores.dtype),
        in_specs=[VMEM],
        out_specs=VMEM,
        compiler_params=PARAMS,
        cost_estimate=cost(0, cores.size * 4),
    )(cores)
    shape = jax.ShapeDtypeStruct((size, cols), jnp.float32)
    estimate = cost(4 * size * cols * rank, size * cols * 8)
    result = None
    for level in range(count - 1, 0, -1):
        if result is None:
            kernel, operands = first_kernel, (noise, self_mob.reshape(size // lanes, lanes))
        else:
            kernel, operands = next_kernel, (result,)
        operands += (bases, mixer, *parts[level])
        result = pl.pallas_call(
            functools.partial(kernel, level),
            out_shape=shape,
            in_specs=[VMEM] * len(operands),
            out_specs=VMEM,
            compiler_params=PARAMS,
            cost_estimate=estimate,
        )(*operands)
    if result is None:
        result = self_mob[:, None] * f32(noise)
    folded = pl.pallas_call(
        functools.partial(fold_kernel, 0),
        out_shape=jax.ShapeDtypeStruct((size, 2 * rank), jnp.bfloat16),
        in_specs=[VMEM, VMEM],
        out_specs=VMEM,
        compiler_params=PARAMS,
        cost_estimate=cost(2 * size * rank * rank, size * rank * 6),
    )(bases, mixer)
    operands = (result, folded, *parts[0])
    return pl.pallas_call(
        last_kernel,
        out_shape=shape,
        in_specs=[VMEM] * len(operands),
        out_specs=ANY,
        scratch_shapes=[pltpu.VMEM((size, cols), jnp.float32), pltpu.SemaphoreType.DMA((CHUNKS,))],
        compiler_params=PARAMS,
        cost_estimate=estimate,
    )(*operands)


def solution(mesh):
    in_specs = (
        P(("groups", "rows", "sub"), "cols"),
        P(None, ("groups", "rows", "sub"), None),
        P("groups", None, None),
        P(("groups", "rows", "sub")),
    )
    out_specs = P(("groups", "rows", "sub"), "cols")
    return jax.shard_map(
        per_device, mesh=mesh, in_specs=in_specs, out_specs=out_specs, check_vma=False
    )
```

```python
import functools

import jax
import jax.numpy as jnp
from jax import lax
from jax.experimental import pallas as pl
from jax.experimental.pallas import tpu as pltpu
from jax.sharding import PartitionSpec as P

VMEM = pl.BlockSpec(memory_space=pltpu.VMEM)
HBM = pl.BlockSpec(memory_space=pltpu.HBM)
ANY = pl.BlockSpec(memory_space=pl.ANY)
PARAMS = pltpu.CompilerParams(vmem_limit_bytes=8 * 2**20)
CHUNKS = 4


def f32(value):
    return value.astype(jnp.float32)


def cost(flops, bytes_accessed):
    return pl.CostEstimate(flops=flops, bytes_accessed=bytes_accessed, transcendentals=0)


def exchange(value, low_mask, high_mask, col_mask, odd_mask=None):
    rows, subs, cols = (lax.axis_size(axis) for axis in ("rows", "sub", "cols"))
    pairs = []
    for i in range(rows * subs * cols):
        low, odd = i < rows * subs * cols // 2, i // cols % subs % 2
        row_mask, sub_mask = low_mask if low else odd_mask if odd and odd_mask else high_mask
        pairs.append((i, i ^ ((row_mask * subs + sub_mask) * cols + col_mask)))
    return lax.ppermute(value, ("rows", "sub", "cols"), pairs)


def project_onto(noise, basis):
    return lax.dot_general(
        noise, basis, (((0,), (0,)), ((), ())), preferred_element_type=jnp.float32
    )


def load_kernel(noise_hbm, bases_hbm, noise_ref, bases_ref, out_ref, wide_ref, sems):
    count = bases_ref.shape[0]
    copies = [pltpu.make_async_copy(noise_hbm, noise_ref, sems.at[count])]
    copies += [
        pltpu.make_async_copy(bases_hbm.at[level], bases_ref.at[level], sems.at[level])
        for level in range(count)
    ]
    for copy in copies:
        copy.start()
    copies[0].wait()
    turned = noise_ref[...].T
    copies[1].wait()
    proj = jnp.dot(turned, bases_ref[0], preferred_element_type=jnp.float32)
    out_ref[...] = proj.astype(out_ref.dtype)
    wide_ref[...] = proj
    for copy in copies[2:]:
        copy.wait()


def load(noise, bases):
    size, cols = noise.shape
    count, _, rank = bases.shape
    return pl.pallas_call(
        load_kernel,
        out_shape=(
            jax.ShapeDtypeStruct(noise.shape, noise.dtype),
            jax.ShapeDtypeStruct(bases.shape, bases.dtype),
            jax.ShapeDtypeStruct((cols, rank), jnp.bfloat16),
            jax.ShapeDtypeStruct((cols, rank), jnp.float32),
        ),
        in_specs=[HBM, HBM],
        out_specs=(VMEM, VMEM, VMEM, VMEM),
        scratch_shapes=[pltpu.SemaphoreType.DMA((count + 1,))],
        compiler_params=PARAMS,
        cost_estimate=cost(2 * size * cols * rank, 2 * size * (cols + count * rank)),
    )(
        pltpu.with_memory_space_constraint(noise, pltpu.HBM),
        pltpu.with_memory_space_constraint(bases, pltpu.HBM),
    )


def project_kernel(level, noise_ref, bases_ref, out_ref):
    out_ref[...] = project_onto(noise_ref[...], bases_ref[level]).astype(out_ref.dtype)


def project(noise, bases, level):
    size, cols = noise.shape
    rank = bases.shape[2]
    return pl.pallas_call(
        functools.partial(project_kernel, level),
        out_shape=jax.ShapeDtypeStruct((cols, rank), jnp.bfloat16),
        in_specs=[VMEM, VMEM],
        out_specs=VMEM,
        compiler_params=PARAMS,
        cost_estimate=cost(2 * size * cols * rank, 2 * size * (cols + rank)),
    )(noise, bases)


def mixer_kernel(depth, cores_ref, out_ref):
    place = lax.axis_index("rows")
    for level in range(out_ref.shape[0]):
        node = place // 2 ** (depth - level - 1)
        core = cores_ref[2**level - 1 + node // 2]

        @pl.when(node % 2 == 1)
        def _():
            out_ref[level] = core

        @pl.when(node % 2 == 0)
        def _():
            out_ref[level] = core.T


def halves(value):
    high = value.astype(jnp.bfloat16)
    return jnp.concatenate([high, (value - f32(high)).astype(jnp.bfloat16)], axis=0)


def mapped(mixer, part_refs):
    total = f32(part_refs[0][...])
    for ref in part_refs[1:]:
        total = total + f32(ref[...])
    both = jnp.dot(halves(total), mixer, preferred_element_type=jnp.float32)
    cols = total.shape[0]
    return halves(both[:cols] + both[cols:])


def spread(basis, weights):
    both = lax.dot_general(
        basis, weights, (((1,), (1,)), ((), ())), preferred_element_type=jnp.float32
    )
    cols = weights.shape[0] // 2
    return both[:, :cols] + both[:, cols:]


def first_kernel(level, noise_ref, mob_ref, bases_ref, mixer_ref, *refs):
    part_refs, out_ref = refs[:-1], refs[-1]
    weights = mapped(mixer_ref[level], part_refs)
    mob = mob_ref[...].T
    rows = mob.shape[0]
    for i in range(mob.shape[1]):
        part = pl.ds(i * rows, rows)
        out_ref[part, :] = mob[:, i : i + 1] * f32(noise_ref[part, :]) + spread(
            bases_ref[level, part, :], weights
        )


def next_kernel(level, sum_ref, bases_ref, mixer_ref, *refs):
    part_refs, out_ref = refs[:-1], refs[-1]
    out_ref[...] = sum_ref[...] + spread(bases_ref[level], mapped(mixer_ref[level], part_refs))


def fold_kernel(level, bases_ref, mixer_ref, out_ref):
    rank = bases_ref.shape[2]
    folded = lax.dot_general(
        bases_ref[level], mixer_ref[level], (((1,), (1,)), ((), ())), preferred_element_type=jnp.float32
    )
    high = folded.astype(jnp.bfloat16)
    out_ref[:, pl.ds(0, rank)] = high
    out_ref[:, pl.ds(rank, rank)] = (folded - f32(high)).astype(jnp.bfloat16)


def last_kernel(sum_ref, folded_ref, part_ref, out_hbm, buf, sems):
    part = part_ref[...]
    both = jnp.concatenate([part, part], axis=1)
    rows = buf.shape[0] // CHUNKS
    copies = []
    for i in range(CHUNKS):
        here = pl.ds(i * rows, rows)
        buf[here, :] = sum_ref[here, :] + lax.dot_general(
            folded_ref[here, :], both, (((1,), (1,)), ((), ())), preferred_element_type=jnp.float32
        )
        copies.append(pltpu.make_async_copy(buf.at[here], out_hbm.at[here], sems.at[i]))
        copies[-1].start()
    for copy in copies:
        copy.wait()


def gather(level, proj, wide, depth, sub_bits):
    swap = 2 ** (depth - level - 1)
    bits = [(0, 2**b) for b in range(sub_bits)] + [(2**b, 0) for b in range(depth - level - 1)]
    if level > 0 and len(bits) < 2:
        masks = [(swap ^ row_mask, sub_mask) for row_mask, sub_mask in [(0, 0)] + bits]
        return [exchange(proj, mask, mask, 0) for mask in masks]
    flip = lax.axis_size("cols") - 1
    total = exchange(wide, (0, 0), (0, 0), flip) if flip else wide
    value, cross, step = proj, flip, 0
    while bits:
        now, bits = bits[:2], bits[2:]
        low = high = now
        if len(now) == 2:
            both = (now[0][0] ^ now[1][0], now[0][1] ^ now[1][1])
            low, high = (both, now[1], now[0]), (now[0], both, now[1])
        terms = [f32(exchange(value, *masks, cross)) for masks in zip(low, high)]
        total = sum(terms[1:], terms[0]) + f32(total)
        value, cross = total, 0
        step += 1
    mask, odd_mask = (swap, 0), (swap + swap // 2, 0)
    return [exchange(f32(total).astype(jnp.bfloat16), mask, mask, flip, odd_mask)]


def per_device(noise, bases, cores, self_mob):
    depth = lax.axis_size("rows").bit_length() - 1
    sub_bits = lax.axis_size("sub").bit_length() - 1
    size, cols = noise.shape
    count, _, rank = bases.shape
    lanes = 128
    noise, bases, first, wide = load(noise, bases)
    parts = []
    for level in range(count):
        proj = project(noise, bases, level) if level else first
        parts.append(gather(level, proj, proj if level else wide, depth, sub_bits))
    mixer = pl.pallas_call(
        functools.partial(mixer_kernel, depth),
        out_shape=jax.ShapeDtypeStruct((count, *cores.shape[1:]), cores.dtype),
        in_specs=[VMEM],
        out_specs=VMEM,
        compiler_params=PARAMS,
        cost_estimate=cost(0, cores.size * 4),
    )(cores)
    shape = jax.ShapeDtypeStruct((size, cols), jnp.float32)
    estimate = cost(4 * size * cols * rank, size * cols * 8)
    result = None
    for level in range(count - 1, 0, -1):
        if result is None:
            kernel, operands = first_kernel, (noise, self_mob.reshape(size // lanes, lanes))
        else:
            kernel, operands = next_kernel, (result,)
        operands += (bases, mixer, *parts[level])
        result = pl.pallas_call(
            functools.partial(kernel, level),
            out_shape=shape,
            in_specs=[VMEM] * len(operands),
            out_specs=VMEM,
            compiler_params=PARAMS,
            cost_estimate=estimate,
        )(*operands)
    if result is None:
        result = self_mob[:, None] * f32(noise)
    folded = pl.pallas_call(
        functools.partial(fold_kernel, 0),
        out_shape=jax.ShapeDtypeStruct((size, 2 * rank), jnp.bfloat16),
        in_specs=[VMEM, VMEM],
        out_specs=VMEM,
        compiler_params=PARAMS,
        cost_estimate=cost(2 * size * rank * rank, size * rank * 6),
    )(bases, mixer)
    operands = (result, folded, *parts[0])
    return pl.pallas_call(
        last_kernel,
        out_shape=shape,
        in_specs=[VMEM] * len(operands),
        out_specs=ANY,
        scratch_shapes=[pltpu.VMEM((size, cols), jnp.float32), pltpu.SemaphoreType.DMA((CHUNKS,))],
        compiler_params=PARAMS,
        cost_estimate=estimate,
    )(*operands)


def solution(mesh):
    in_specs = (
        P(("groups", "rows", "sub"), "cols"),
        P(None, ("groups", "rows", "sub"), None),
        P("groups", None, None),
        P(("groups", "rows", "sub")),
    )
    out_specs = P(("groups", "rows", "sub"), "cols")
    return jax.shard_map(
        per_device, mesh=mesh, in_specs=in_specs, out_specs=out_specs, check_vma=False
    )
```
